128 devices in a mesh: kz: 16 (over y_hi, x, core), pw: 8 (over z, y_lo).
Axes of the slice: x: 4, y: 4 (y_hi: 2, y_lo: 2; y = y_hi * 2 + y_lo), z: 4, core: 2. Of those that a mesh axis runs over, the one named last changes fastest.
Arguments:
- states: bfloat16 [16, 2, 384, 1024, 128], P('kz', None, None, 'pw'), may hold values from -1 to 1
- stick_perm: int32 [1024], P('pw'), may hold values from 0 to 1023, as said below
Outputs:
- margin: float32 [384, 16, 2, 384], P('pw', 'kz')
The draws below stay inside these ranges and needn't reach their ends.
Inputs may be any that keep to these rules, and one draw needn't show every extreme that they name: `stick_perm`: each aligned run of 128 entries, starting at a multiple of 128, is a permutation of the stick numbers of that run.
All inputs are finite; a program needn't handle non-finite values.
Results may differ from the reference program's by a relative error of at most 0.0003.
Values may be sent and summed in bfloat16 or wider, within the bound.
No kernel may reach another device: no remote copies, remote signals or barrier semaphores. Data moves between devices by JAX's collectives and lax.ppermute only.
A program may use at most 192 MiB of HBM per device.

```python
import jax
import jax.numpy as jnp
from jax import lax

NB = 384
SL = 128
SDEV = 128
NK = 16
NSTICK = 1024
NPW = 131072


def one_block(block_key):
    return jax.random.permutation(block_key, SDEV)


def draw_stick_perm(key, part):
    blocks = NSTICK // SDEV
    keys = jax.random.split(key, blocks)
    perms = jax.vmap(one_block)(keys).astype(jnp.int32)
    offsets = (jnp.arange(blocks, dtype=jnp.int32) * SDEV)[:, None]
    return (perms + offsets).reshape(NSTICK)


def raised(entries, stream_key, source, target, blocks, factor):
    def block_of(axis_at):
        return (jnp.arange(entries.shape[axis_at]) // (entries.shape[axis_at] // blocks)).reshape((-1,) + (1,) * (entries.ndim - 1 - axis_at))

    one_side = jax.random.permutation(stream_key, blocks)[block_of(target)]
    second = (block_of(target) + blocks // 2) % blocks
    return jnp.where((block_of(source) == one_side) | (block_of(source) == second), factor * entries, entries)


def levels(rng, extent, cuts, smallest, high):
    factor_of = 1.0
    for axis_at, parts in cuts:
        heights = jax.random.uniform(jax.random.fold_in(jax.random.fold_in(rng, 6), axis_at), (parts,), jnp.float32, smallest / len(cuts), high / len(cuts))
        factor_of = factor_of * jnp.repeat(jnp.exp(heights), extent[axis_at] // parts).reshape((-1,) + (1,) * (len(extent) - 1 - axis_at))
    return factor_of


def bell_draw_with(own_key, dims, width, reach, cuts, heavy, kind=jnp.bfloat16):
    array = width * jax.random.normal(own_key, dims, jnp.float32)
    if cuts:
        array = array * levels(own_key, dims, cuts, -0.22, 0.18)
    return jnp.clip(raised(array, jax.random.fold_in(own_key, 3), *heavy), -reach, reach).astype(kind)


def setup_inputs(seed: int = 0) -> dict:
    key_of = jax.random.split(jax.random.key(seed), 3)
    states = bell_draw_with(key_of[0], (NK, 2, NB, NSTICK, SL), (NPW ** -0.25), 1.0, ((0, 16), (3, 8)), (3, 2, 8, 2.0))
    stick_perm = draw_stick_perm(jax.random.fold_in(key_of[2], 71), 0)
    return dict(states=states, stick_perm=stick_perm)


def wrap_shift(state, perm):
    moved = jnp.take(state, perm, axis=2)
    return jnp.concatenate([moved[..., 1:], jnp.zeros_like(moved[..., :1])], axis=-1)


def pair_margin(left_state, right_state):
    left_flat = left_state.astype(jnp.float32).reshape(2, NB, -1)
    right_flat = right_state.astype(jnp.float32).reshape(2, NB, -1)
    products = jnp.einsum("amp,bnp->mabn", left_flat, right_flat, precision=lax.Precision.HIGHEST)
    real_part = products[:, 0, 0] + products[:, 1, 1]
    imag_part = products[:, 0, 1] - products[:, 1, 0]
    return jnp.stack([real_part, imag_part], axis=1)


def reference(states, stick_perm):
    wrapped = wrap_shift(states[0], stick_perm)

    def one_point(index):
        left_state = lax.dynamic_index_in_dim(states, index, 0, keepdims=False)
        following = lax.dynamic_index_in_dim(states, (index + 1) % NK, 0, keepdims=False)
        right_state = jnp.where(index == NK - 1, wrapped, following)
        return pair_margin(left_state, right_state)

    result = lax.map(one_point, jnp.arange(NK, dtype=jnp.int32))
    return jnp.transpose(result, (1, 0, 2, 3))
```

```python
import jax
import jax.numpy as jnp
from jax import lax
from jax.experimental import pallas as pl
from jax.experimental.pallas import tpu as pltpu
from jax.sharding import PartitionSpec as P

SUB = 64
LANES = 128
PITCH = SUB + 1
CHUNKS = ((0, 1, (64,)), (1, 1, (64,)), (2, 2, (64,)), (4, 2, (48, 16)))
GROUPS = ((0, 1), (2,), (3,))
STEP = 16
PARAMS = pltpu.CompilerParams(vmem_limit_bytes=56 << 20)


def shifted(value, axis, steps):
    count = lax.axis_size(axis)
    return lax.ppermute(value, axis, [(s, (s + steps) % count) for s in range(count)])


def relayout(states, perm, wraps, chunk, left):
    first, units, pieces = chunk
    sticks = states.shape[2]
    half = sticks // 2
    bands = units * SUB

    def body(perm_ref, wraps_ref, x_ref, *refs):
        outs, scratch = refs[:-1], refs[-1]
        x = x_ref.at[0]
        for m in range(SUB):
            row = x[m] if left else x[m // 8, m % 8]
            scratch[pl.ds(m, sticks, stride=PITCH), :] = row.astype(jnp.float32)

        def put(s, value):
            value = value.astype(jnp.bfloat16)
            sent = s < half if left else s >= half
            if not sent:
                outs[-1][0, s % half] = value
                return
            at = s % half
            for piece, size in enumerate(pieces):
                if at < size:
                    outs[piece][0, at] = value
                    return
                at -= size

        def plain():
            for s in range(sticks):
                put(s, scratch[pl.ds(s * PITCH, SUB), :])

        def wrapped():
            keep = lax.broadcasted_iota(jnp.int32, (SUB, LANES), 1) < LANES - 1
            for s in range(sticks):
                value = scratch[pl.ds(perm_ref[s] * PITCH, SUB), :]
                put(s, jnp.where(keep, pltpu.roll(value, LANES - 1, 1), 0.0))

        if left:
            pl.when(wraps_ref[0] == 0)(plain)
            pl.when(wraps_ref[0] != 0)(wrapped)
        else:
            plain()

    if left:
        view = states
        in_spec = pl.BlockSpec((1, SUB, sticks, LANES), lambda c, g, *_: (c, first + g, 0, 0))
    else:
        view = states.reshape(2, 8, states.shape[1] // 8, sticks, LANES)
        in_spec = pl.BlockSpec((1, 8, 8, sticks, LANES), lambda c, g, *_: (c, 0, first + g, 0, 0))
    sizes = (*pieces, half)
    return pl.pallas_call(
        body,
        grid_spec=pltpu.PrefetchScalarGridSpec(
            num_scalar_prefetch=2,
            grid=(2, units),
            in_specs=[in_spec],
            out_specs=[pl.BlockSpec((1, n, SUB, LANES), lambda c, g, *_: (c, 0, g, 0)) for n in sizes],
            scratch_shapes=[pltpu.VMEM((sticks * PITCH, LANES), jnp.float32)],
        ),
        out_shape=[jax.ShapeDtypeStruct((2, n, bands, LANES), jnp.bfloat16) for n in sizes],
        compiler_params=PARAMS,
        name="relayout_left" if left else "relayout_right",
    )(perm, wraps, view)


def products(rows, columns, offset_rows, offset_columns, sticks, start, finish):
    n_rows = sum(r.shape[2] for r in rows)
    n_columns = sum(c.shape[2] for c in columns)
    shape = (2 * n_rows, 2 * n_columns)
    steps = sticks // STEP

    def side(refs):
        return jnp.concatenate(
            [jnp.concatenate([r[c, j] for j in range(STEP)], -1) for c in range(2) for r in refs], 0
        )

    def body(*refs):
        row_refs, refs = refs[: len(rows)], refs[len(rows) :]
        column_refs, refs = refs[: len(columns)], refs[len(columns) :]
        start_ref = None
        if start is not None:
            start_ref, refs = refs[0], refs[1:]
        out, total = refs
        step = pl.program_id(0)
        new = lax.dot_general(
            side(row_refs), side(column_refs), (((1,), (1,)), ((), ())), preferred_element_type=jnp.float32
        )

        @pl.when(step == 0)
        def _():
            total[...] = new if start_ref is None else start_ref[...] + new

        @pl.when(step > 0)
        def _():
            total[...] += new

        @pl.when(step == steps - 1)
        def _():
            if not finish:
                out[...] = total[...]
                return
            real = total[:n_rows, :n_columns] + total[n_rows:, n_columns:]
            imag = total[:n_rows, n_columns:] - total[n_rows:, :n_columns]
            for u in range(n_rows // SUB):
                for q in range(8):
                    at = u * SUB + q * 8
                    out[q, 0, 8 * u : 8 * u + 8] = real[at : at + 8]
                    out[q, 1, 8 * u : 8 * u + 8] = imag[at : at + 8]

    def spec(array, offset):
        return pl.BlockSpec((2, STEP, array.shape[2], LANES), lambda s: (0, offset + s, 0, 0))

    in_specs = [spec(r, offset_rows // STEP) for r in rows] + [spec(c, offset_columns // STEP) for c in columns]
    operands = [*rows, *columns]
    if start is not None:
        in_specs.append(pl.BlockSpec(shape, lambda s: (0, 0)))
        operands.append(start)
    out_shape = (8, 2, n_rows // 8, n_columns) if finish else shape
    return pl.pallas_call(
        body,
        grid=(steps,),
        in_specs=in_specs,
        out_specs=pl.BlockSpec(out_shape, lambda s: (0,) * len(out_shape)),
        out_shape=jax.ShapeDtypeStruct(out_shape, jnp.float32),
        scratch_shapes=[pltpu.VMEM(shape, jnp.float32)],
        compiler_params=PARAMS,
        name="products",
    )(*operands)


def shards(states, stick_perm):
    states = states[0]
    sticks = states.shape[2]
    perm = stick_perm - lax.axis_index("pw") * sticks
    wraps = (lax.axis_index("kz") == 0).astype(jnp.int32).reshape(1)
    from_right, from_left, own_rows, own_columns = [], [], [], []
    for chunk in CHUNKS:
        *sent, kept = relayout(states, perm, wraps, chunk, True)
        wraps, kept = lax.optimization_barrier((wraps, kept))
        own_columns.append(kept)
        from_right.append([shifted(piece, "kz", -1) for piece in sent])
        *sent, kept = relayout(states, perm, wraps, chunk, False)
        wraps, kept = lax.optimization_barrier((wraps, kept))
        own_rows.append(kept)
        from_left.append([shifted(piece, "kz", 1) for piece in sent])

    left_parts, right_parts = [], []
    for group in GROUPS:
        pieces = CHUNKS[group[0]][2]
        right_total = left_total = None
        offset = 0
        for index, size in enumerate(pieces):
            last = index == len(pieces) - 1
            right_total = products(
                [from_left[c][index] for c in group], own_columns, 0, offset, size, right_total, last
            )
            left_total = products(
                own_rows, [from_right[c][index] for c in group], offset, 0, size, left_total, last
            )
            offset += size
        own_rows, own_columns, right_total, left_total = lax.optimization_barrier(
            (own_rows, own_columns, right_total, left_total)
        )
        mine = lax.all_to_all(right_total, "pw", 0, 0, tiled=True).sum(0)
        right_parts.append(shifted(mine, "kz", -1))
        left_parts.append(lax.all_to_all(left_total, "pw", 0, 0, tiled=True).sum(0))
    margin = jnp.concatenate(left_parts, 2) + jnp.concatenate(right_parts, 1)
    return jnp.transpose(margin, (1, 0, 2))[:, None]


def solution(mesh):
    in_specs = (P("kz", None, None, "pw", None), P("pw"))
    out_specs = P("pw", "kz", None, None)
    return jax.shard_map(shards, mesh=mesh, in_specs=in_specs, out_specs=out_specs, check_vma=False)
```

```python
import jax
import jax.numpy as jnp
from jax import lax
from jax.experimental import pallas as pl
from jax.experimental.pallas import tpu as pltpu
from jax.sharding import PartitionSpec as P

SUB = 64
LANES = 128
PITCH = SUB + 1
CHUNKS = ((0, 1, (64,)), (1, 1, (64,)), (2, 2, (64,)), (4, 2, (48, 16)))
GROUPS = ((0, 1), (2,), (3,))
STEP = 16
RELAYOUT_COST = 5_000_000_000
PRODUCT_COST = 3
PARAMS = pltpu.CompilerParams(vmem_limit_bytes=56 << 20)


def shifted(value, axis, steps):
    count = lax.axis_size(axis)
    return lax.ppermute(value, axis, [(s, (s + steps) % count) for s in range(count)])


def relayout(states, perm, wraps, chunk, left):
    first, units, pieces = chunk
    sticks = states.shape[2]
    half = sticks // 2
    bands = units * SUB

    def body(perm_ref, wraps_ref, x_ref, *refs):
        outs, scratch = refs[:-1], refs[-1]
        x = x_ref.at[0]
        for m in range(SUB):
            row = x[m] if left else x[m // 8, m % 8]
            scratch[pl.ds(m, sticks, stride=PITCH), :] = row.astype(jnp.float32)

        def put(s, value):
            value = value.astype(jnp.bfloat16)
            sent = s < half if left else s >= half
            if not sent:
                outs[-1][0, s % half] = value
                return
            at = s % half
            for piece, size in enumerate(pieces):
                if at < size:
                    outs[piece][0, at] = value
                    return
                at -= size

        def plain():
            for s in range(sticks):
                put(s, scratch[pl.ds(s * PITCH, SUB), :])

        def wrapped():
            keep = lax.broadcasted_iota(jnp.int32, (SUB, LANES), 1) < LANES - 1
            for s in range(sticks):
                value = scratch[pl.ds(perm_ref[s] * PITCH, SUB), :]
                put(s, jnp.where(keep, pltpu.roll(value, LANES - 1, 1), 0.0))

        if left:
            pl.when(wraps_ref[0] == 0)(plain)
            pl.when(wraps_ref[0] != 0)(wrapped)
        else:
            plain()

    if left:
        view = states
        in_spec = pl.BlockSpec((1, SUB, sticks, LANES), lambda c, g, *_: (c, first + g, 0, 0))
    else:
        view = states.reshape(2, 8, states.shape[1] // 8, sticks, LANES)
        in_spec = pl.BlockSpec((1, 8, 8, sticks, LANES), lambda c, g, *_: (c, 0, first + g, 0, 0))
    sizes = (*pieces, half)
    return pl.pallas_call(
        body,
        grid_spec=pltpu.PrefetchScalarGridSpec(
            num_scalar_prefetch=2,
            grid=(2, units),
            in_specs=[in_spec],
            out_specs=[pl.BlockSpec((1, n, SUB, LANES), lambda c, g, *_: (c, 0, g, 0)) for n in sizes],
            scratch_shapes=[pltpu.VMEM((sticks * PITCH, LANES), jnp.float32)],
        ),
        out_shape=[jax.ShapeDtypeStruct((2, n, bands, LANES), jnp.bfloat16) for n in sizes],
        compiler_params=PARAMS,
        cost_estimate=pl.CostEstimate(flops=RELAYOUT_COST * units, transcendentals=0, bytes_accessed=8 * bands * sticks * LANES),
        name="relayout_left" if left else "relayout_right",
    )(perm, wraps, view)


def products(left, right, start, finish):
    sides = (left, right)
    steps = left[3] // STEP
    heights = [sum(r.shape[2] for r in rows) for rows, *_ in sides]
    widths = [sum(c.shape[2] for c in columns) for _, columns, *_ in sides]
    shapes = [(2 * h, 2 * w) for h, w in zip(heights, widths)]

    def stack(refs):
        return jnp.concatenate(
            [jnp.concatenate([r[c, j] for j in range(STEP)], -1) for c in range(2) for r in refs], 0
        )

    def body(*refs):
        refs = list(refs)
        take = lambda n: [refs.pop(0) for _ in range(n)]
        operands = [(take(len(rows)), take(len(columns))) for rows, columns, *_ in sides]
        starts = take(2) if start else None
        outs = take(1) if finish else take(2)
        totals = take(2)
        step = pl.program_id(0)
        for side, (rows, columns) in enumerate(operands):
            new = lax.dot_general(
                stack(rows), stack(columns), (((1,), (1,)), ((), ())), preferred_element_type=jnp.float32
            )

            @pl.when(step == 0)
            def _():
                totals[side][...] = starts[side][...] + new if start else new

            @pl.when(step > 0)
            def _():
                totals[side][...] += new

        @pl.when(step == steps - 1)
        def _():
            for side in range(2):
                total, h, w = totals[side], heights[side], widths[side]
                if not finish:
                    outs[side][...] = total[...]
                    continue
                real = total[:h, :w] + total[h:, w:]
                imag = total[:h, w:] - total[h:, :w]
                for part, value in enumerate((real, imag)):
                    for u in range(h // SUB):
                        for q in range(8):
                            block = value[u * SUB + q * 8 : u * SUB + q * 8 + 8]
                            for n in range(w // LANES):
                                at = (n * (h // SUB) + u) * 8
                                outs[0][q, side, part, at : at + 8] = block[:, n * LANES : (n + 1) * LANES]

    def spec(array, offset):
        return pl.BlockSpec((2, STEP, array.shape[2], LANES), lambda s: (0, offset // STEP + s, 0, 0))

    in_specs, operands = [], []
    for rows, columns, (row_offset, column_offset), _ in sides:
        in_specs += [spec(r, row_offset) for r in rows] + [spec(c, column_offset) for c in columns]
        operands += [*rows, *columns]
    whole = [pl.BlockSpec(shape, lambda s: (0, 0)) for shape in shapes]
    if start:
        in_specs += whole
        operands += start
    if finish:
        out_shape = [(8, 2, 2, 48, LANES)]
        out_specs = [pl.BlockSpec(out_shape[0], lambda s: (0, 0, 0, 0, 0))]
    else:
        out_shape, out_specs = shapes, whole
    return pl.pallas_call(
        body,
        grid=(steps,),
        in_specs=in_specs,
        out_specs=out_specs,
        out_shape=[jax.ShapeDtypeStruct(shape, jnp.float32) for shape in out_shape],
        scratch_shapes=[pltpu.VMEM(shape, jnp.float32) for shape in shapes],
        compiler_params=PARAMS,
        cost_estimate=pl.CostEstimate(
            flops=PRODUCT_COST * 2 * steps * STEP * LANES * sum(h * w for h, w in shapes),
            transcendentals=0,
            bytes_accessed=4 * steps * STEP * LANES * sum(h + w for h, w in shapes),
        ),
        name="products",
    )(*operands)


def after(value, *others):
    return lax.optimization_barrier((value, others))[0]


def reduced(total):
    return lax.all_to_all(total, "pw", 0, 0, tiled=True).sum(0)


def reduced_in_two(total):
    count = lax.axis_size("pw")
    groups = [list(range(p, count, 2)) for p in range(2)]
    halves = total.reshape(count // 2, 2, *total.shape[1:])
    halves = lax.all_to_all(halves, "pw", 0, 0, axis_index_groups=groups, tiled=True).sum(0)
    side = lax.axis_index("pw") % 2
    kept = lax.dynamic_index_in_dim(halves, side, 0, keepdims=False)
    sent = lax.dynamic_index_in_dim(halves, 1 - side, 0, keepdims=False)
    return kept + lax.ppermute(sent, "pw", [(p, p ^ 1) for p in range(count)])


def shards(states, stick_perm):
    states = states[0]
    sticks = states.shape[2]
    perm = stick_perm - lax.axis_index("pw") * sticks
    token = (lax.axis_index("kz") == 0).astype(jnp.int32).reshape(1)
    columns, rows, from_right, from_left = [], [], [], []
    for index, chunk in enumerate(CHUNKS):
        for left in (True, False):
            if index > 1:
                token = after(token, (from_right if left else from_left)[index - 2][0])
            *sent, kept = relayout(states, perm, token, chunk, left)
            token, kept = lax.optimization_barrier((token, kept))
            (columns if left else rows).append(kept)
            for piece in range(1, len(sent)):
                sent[piece] = after(sent[piece], (from_right if left else from_left)[index - 1][0])
            (from_right if left else from_left).append([shifted(p, "kz", -1 if left else 1) for p in sent])

    left_parts, right_parts = [], []
    for group in GROUPS:
        offset, totals = 0, None
        pieces = CHUNKS[group[0]][2]
        for index, size in enumerate(pieces):
            last = index == len(pieces) - 1
            arrived = [[side[c][index] for c in group] for side in (from_right, from_left)]
            if index:
                arrived, left_parts, right_parts = lax.optimization_barrier((arrived, left_parts, right_parts))
            totals = products(
                (rows, arrived[0], (offset, 0), size), (arrived[1], columns, (0, offset), size), totals, last
            )
            offset += size
        rows, columns, totals = lax.optimization_barrier((rows, columns, totals))
        mine = reduced(totals[0]) if group == GROUPS[-1] else reduced_in_two(totals[0])
        left_parts.append(mine[0])
        right_parts.append(shifted(mine[1], "kz", -1))
    right_parts = [jnp.concatenate([r[:, 16 * n : 16 * n + 16] for n in range(3)], 2) for r in right_parts]
    margin = jnp.concatenate(left_parts, 2) + jnp.concatenate(right_parts, 1)
    return jnp.transpose(margin, (1, 0, 2))[:, None]


def solution(mesh):
    in_specs = (P("kz", None, None, "pw", None), P("pw"))
    out_specs = P("pw", "kz", None, None)
    return jax.shard_map(shards, mesh=mesh, in_specs=in_specs, out_specs=out_specs, check_vma=False)
```

```python
import jax
import jax.numpy as jnp
from jax import lax
from jax.experimental import pallas as pl
from jax.experimental.pallas import tpu as pltpu
from jax.sharding import PartitionSpec as P

LANES = 128
CHUNKS = ((0, 64, 1, (64,)), (64, 64, 1, (64,)), (128, 64, 2, (64,)), (256, 64, 2, (48, 16)))
GROUPS = ((0, 1), (2,), (3,))
STEP = 16
RELAYOUT_COST = 5_000_000_000
PRODUCT_COST = 3
TAIL = 16
PARAMS = pltpu.CompilerParams(vmem_limit_bytes=56 << 20)


def shifted(value, axis, steps):
    count = lax.axis_size(axis)
    return lax.ppermute(value, axis, [(s, (s + steps) % count) for s in range(count)])


def relayout(states, perm, wraps, chunk, left):
    first, sub, units, pieces = chunk
    pitch = sub + 1
    each = sub // 8
    sticks = states.shape[2]
    half = sticks // 2
    bands = units * sub

    def body(perm_ref, wraps_ref, x_ref, *refs):
        outs, scratch = refs[:-1], refs[-1]
        x = x_ref.at[0]
        for m in range(sub):
            row = x[m] if left else x[m // each, m % each]
            scratch[pl.ds(m, sticks, stride=pitch), :] = row.astype(jnp.float32)

        def put(s, value):
            value = value.astype(jnp.bfloat16)
            sent = s < half if left else s >= half
            if not sent:
                outs[-2][0, s % half] = value
                if s % half >= half - TAIL:
                    outs[-1][0, s % half - (half - TAIL)] = value
                return
            at = s % half
            for piece, size in enumerate(pieces):
                if at < size:
                    outs[piece][0, at] = value
                    return
                at -= size

        def plain():
            for s in range(sticks):
                put(s, scratch[pl.ds(s * pitch, sub), :])

        def wrapped():
            keep = lax.broadcasted_iota(jnp.int32, (sub, LANES), 1) < LANES - 1
            for s in range(sticks):
                value = scratch[pl.ds(perm_ref[s] * pitch, sub), :]
                put(s, jnp.where(keep, pltpu.roll(value, LANES - 1, 1), 0.0))

        if left:
            pl.when(wraps_ref[0] == 0)(plain)
            pl.when(wraps_ref[0] != 0)(wrapped)
        else:
            plain()

    if left:
        view = states
        in_spec = pl.BlockSpec((1, sub, sticks, LANES), lambda c, g, *_: (c, first // sub + g, 0, 0))
    else:
        view = states.reshape(2, 8, states.shape[1] // 8, sticks, LANES)
        in_spec = pl.BlockSpec((1, 8, each, sticks, LANES), lambda c, g, *_: (c, 0, first // sub + g, 0, 0))
    sizes = (*pieces, half, TAIL)
    return pl.pallas_call(
        body,
        grid_spec=pltpu.PrefetchScalarGridSpec(
            num_scalar_prefetch=2,
            grid=(2, units),
            in_specs=[in_spec],
            out_specs=[pl.BlockSpec((1, n, sub, LANES), lambda c, g, *_: (c, 0, g, 0)) for n in sizes],
            scratch_shapes=[pltpu.VMEM((sticks * pitch, LANES), jnp.float32)],
        ),
        out_shape=[jax.ShapeDtypeStruct((2, n, bands, LANES), jnp.bfloat16) for n in sizes],
        compiler_params=PARAMS,
        cost_estimate=pl.CostEstimate(flops=RELAYOUT_COST * bands // 64, transcendentals=0, bytes_accessed=8 * bands * sticks * LANES),
        name="relayout_left" if left else "relayout_right",
    )(perm, wraps, view)


def products(left, right, units, size, start, finish, resident, cost):
    sides = (left, right)
    steps = 1 if resident else size // STEP
    heights = [sum(r.shape[2] for r in rows) for rows, _ in sides]
    widths = [sum(c.shape[2] for c in columns) for _, columns in sides]
    shapes = [(2 * h, 2 * w) for h, w in zip(heights, widths)]

    def stack(refs):
        return jnp.concatenate(
            [jnp.concatenate([r[c, j] for j in range(STEP)], -1) for c in range(2) for r in refs], 0
        )

    def body(*refs):
        refs = list(refs)
        take = lambda n: [refs.pop(0) for _ in range(n)]
        operands = [(take(len(rows)), take(len(columns))) for rows, columns in sides]
        starts = take(2) if start else None
        outs = take(1) if finish else take(2)
        totals = take(2)
        step = pl.program_id(0)

        @pl.when(step == 0)
        def _():
            for side in range(2):
                totals[side][...] = starts[side][...] if start else jnp.zeros(shapes[side], jnp.float32)

        for side, (rows, columns) in enumerate(operands):
            totals[side][...] += lax.dot_general(
                stack(rows), stack(columns), (((1,), (1,)), ((), ())), preferred_element_type=jnp.float32
            )

        @pl.when(step == steps - 1)
        def _():
            for side in range(2):
                total, h, w = totals[side], heights[side], widths[side]
                if not finish:
                    outs[side][...] = total[...]
                    continue
                real = total[:h, :w] + total[h:, w:]
                imag = total[:h, w:] - total[h:, :w]
                for part, value in enumerate((real, imag)):
                    at, to = 0, 0
                    for unit in units[side]:
                        each = unit // 8
                        for q in range(8):
                            block = value[at : at + each]
                            at += each
                            for n in range(w // LANES):
                                into = n * (h // 8) + to
                                outs[0][q, side, part, into : into + each] = block[:, n * LANES : (n + 1) * LANES]
                        to += each

    def spec(array):
        if resident:
            return pl.BlockSpec(memory_space=pltpu.VMEM)
        return pl.BlockSpec((2, STEP, array.shape[2], LANES), lambda s: (0, s, 0, 0))

    in_specs, operands = [], []
    for rows, columns in sides:
        in_specs += [spec(r) for r in (*rows, *columns)]
        operands += [*rows, *columns]
    whole = [pl.BlockSpec(shape, lambda s: (0, 0)) for shape in shapes]
    if start:
        in_specs += [pl.BlockSpec(memory_space=pltpu.VMEM)] * 2
        operands += start
    if finish:
        out_shape = [(8, 2, 2, 48, LANES)]
        out_specs = [pl.BlockSpec(out_shape[0], lambda s: (0, 0, 0, 0, 0))]
    else:
        out_shape, out_specs = shapes, whole
    return pl.pallas_call(
        body,
        grid=(steps,),
        in_specs=in_specs,
        out_specs=out_specs,
        out_shape=[jax.ShapeDtypeStruct(shape, jnp.float32) for shape in out_shape],
        scratch_shapes=[pltpu.VMEM(shape, jnp.float32) for shape in shapes],
        compiler_params=pltpu.CompilerParams(vmem_limit_bytes=(20 if resident else 56) << 20),
        cost_estimate=pl.CostEstimate(
            flops=cost * 2 * steps * STEP * LANES * sum(h * w for h, w in shapes),
            transcendentals=0,
            bytes_accessed=4 * steps * STEP * LANES * sum(h + w for h, w in shapes),
        ),
        name="products",
    )(*operands)


def after(value, *others):
    return lax.optimization_barrier((value, others))[0]


def summed(total):
    return lax.all_to_all(total, "pw", 0, 0, tiled=True).sum(0)


def summed_apart(total):
    count = lax.axis_size("pw")
    groups = [list(range(p, count, 2)) for p in range(2)]
    pairs = total.reshape(count // 2, 2, *total.shape[1:])
    return lax.all_to_all(pairs, "pw", 0, 0, axis_index_groups=groups, tiled=True).sum(0)


def summed_near(pairs):
    side = lax.axis_index("pw") % 2
    kept = lax.dynamic_index_in_dim(pairs, side, 1, keepdims=False)
    sent = lax.dynamic_index_in_dim(pairs, 1 - side, 1, keepdims=False)
    return kept + lax.ppermute(sent, "pw", [(p, p ^ 1) for p in range(lax.axis_size("pw"))])


def shards(states, stick_perm):
    states = states[0]
    sticks = states.shape[2]
    perm = stick_perm - lax.axis_index("pw") * sticks
    token = (lax.axis_index("kz") == 0).astype(jnp.int32).reshape(1)
    columns, rows, from_right, from_left = [], [], [], []
    tail_columns, tail_rows = [], []
    for index, chunk in enumerate(CHUNKS):
        for left in (True, False):
            if index > 1:
                token = after(token, (from_right if left else from_left)[index - 2][0])
            *sent, kept, tail = relayout(states, perm, token, chunk, left)
            token, kept = lax.optimization_barrier((token, kept))
            (columns if left else rows).append(kept)
            (tail_columns if left else tail_rows).append(tail)
            for piece in range(1, len(sent)):
                if not left:
                    sent[piece] = after(sent[piece], from_right[index - 1][0])
            (from_right if left else from_left).append([shifted(p, "kz", -1 if left else 1) for p in sent])

    runs = [[chunk[1]] * chunk[2] for chunk in CHUNKS]
    early = []
    for group in GROUPS:
        totals = None
        pieces = CHUNKS[group[0]][3]
        units = (sum(runs, []), sum((runs[c] for c in group), []))
        for index, size in enumerate(pieces):
            last = index == len(pieces) - 1
            arrived = [[side[c][index] for c in group] for side in (from_right, from_left)]
            own = (tail_rows, tail_columns) if index else (rows, columns)
            if index:
                arrived, totals = lax.optimization_barrier((arrived, totals))
            totals = products(
                (own[0], arrived[0]), (arrived[1], own[1]), units, size, totals, last, index > 0, PRODUCT_COST
            )
        rows, columns, totals = lax.optimization_barrier((rows, columns, totals))
        if group != GROUPS[-1]:
            early.append(summed_apart(totals[0]))
    parts = jnp.concatenate([summed_near(jnp.stack(early)), summed(totals[0])[None]])
    groups, _, _, height, _ = parts.shape
    from_left_part = shifted(parts[:, 1], "kz", -1).reshape(groups, 2, groups, height // groups, LANES)
    left = jnp.transpose(parts[:, 0], (2, 1, 0, 3)).reshape(height, 2, groups * LANES)
    right = jnp.transpose(from_left_part, (0, 3, 1, 2, 4)).reshape(height, 2, groups * LANES)
    return (left + right)[:, None]


def solution(mesh):
    in_specs = (P("kz", None, None, "pw", None), P("pw"))
    out_specs = P("pw", "kz", None, None)
    return jax.shard_map(shards, mesh=mesh, in_specs=in_specs, out_specs=out_specs, check_vma=False)
```

```python
import jax
import jax.numpy as jnp
from jax import lax
from jax.experimental import pallas as pl
from jax.experimental.pallas import tpu as pltpu
from jax.sharding import PartitionSpec as P

LANES = 128
CHUNKS = ((0, 64, 1, (64,)), (64, 64, 1, (64,)), (128, 64, 2, (64,)), (256, 64, 2, (48, 16)))
SIDES = (True, False)
GROUPS = ((0, 1), (2,), (3,))
STEPS = {64: 16, 48: 16, 16: 8}
RELAYOUT_COST = 5_000_000_000
PRODUCT_COST = 2
PARAMS = pltpu.CompilerParams(vmem_limit_bytes=56 << 20)


def shifted(value, axis, steps):
    count = lax.axis_size(axis)
    return lax.ppermute(value, axis, [(s, (s + steps) % count) for s in range(count)])


def relayout(states, perm, wraps, chunk, left, own, sends=True):
    first, sub, units, pieces = chunk
    keeps = own is not None
    own = own or ()
    pitch = sub + 1
    each = sub // 8
    sticks = states.shape[2]
    half = sticks // 2
    bands = units * sub
    sent_half, kept_half = (range(half), range(half, sticks)) if left else (range(half, sticks), range(half))
    wanted = [*(sent_half if sends else ()), *(kept_half if keeps else ())]
    low = min(wanted)
    base = 0 if left else low
    pieces = pieces if sends else ()
    halves = (half,) if keeps else ()
    all_bands = states.shape[1]

    def body(perm_ref, wraps_ref, x_ref, *refs):
        outs, scratch = refs[len(own) : -1], refs[-1]

        def spread(start, count):
            for m in range(sub):
                row = x_ref.at[0, m] if left else x_ref.at[0, m // each, m % each]
                row = row[start - base : start - base + count].astype(jnp.float32)
                scratch[pl.ds(start * pitch + m, count, stride=pitch), :] = row

        def put(s, value):
            value = value.astype(jnp.bfloat16)
            at = s % half
            if s in kept_half:
                outs[-1][0, at] = value
                return
            for piece, size in enumerate(pieces):
                if at < size:
                    outs[piece][0, at] = value
                    return
                at -= size

        def plain():
            spread(low, len(wanted))
            for s in wanted:
                put(s, scratch[pl.ds(s * pitch, sub), :])

        def wrapped():
            spread(0, sticks)
            keep = lax.broadcasted_iota(jnp.int32, (sub, LANES), 1) < LANES - 1
            for s in wanted:
                value = scratch[pl.ds(perm_ref[s] * pitch, sub), :]
                put(s, jnp.where(keep, pltpu.roll(value, LANES - 1, 1), 0.0))

        if left:
            pl.when(wraps_ref[0] == 0)(plain)
            pl.when(wraps_ref[0] != 0)(wrapped)
        else:
            plain()

    if left:
        view = states
        in_spec = pl.BlockSpec((1, sub, sticks, LANES), lambda c, g, *_: (c, first // sub + g, 0, 0))
    else:
        view = states.reshape(2, 8, states.shape[1] // 8, sticks, LANES)
        block = (1, 8, each, len(wanted), LANES)
        in_spec = pl.BlockSpec(block, lambda c, g, *_: (c, 0, first // sub + g, low // len(wanted), 0))
    return pl.pallas_call(
        body,
        grid_spec=pltpu.PrefetchScalarGridSpec(
            num_scalar_prefetch=2,
            grid=(2, units),
            in_specs=[in_spec] + [pl.BlockSpec(memory_space=pl.ANY)] * len(own),
            out_specs=[pl.BlockSpec((1, n, sub, LANES), lambda c, g, *_: (c, 0, g, 0)) for n in pieces]
            + [pl.BlockSpec((1, n, sub, LANES), lambda c, g, *_: (c, 0, first // sub + g, 0)) for n in halves],
            scratch_shapes=[pltpu.VMEM((sticks * pitch, LANES), jnp.float32)],
        ),
        out_shape=[jax.ShapeDtypeStruct((2, n, bands, LANES), jnp.bfloat16) for n in pieces]
        + [jax.ShapeDtypeStruct((2, n, all_bands, LANES), jnp.bfloat16) for n in halves],
        input_output_aliases={3 + at: len(pieces) + at for at in range(len(own))},
        compiler_params=PARAMS,
        cost_estimate=pl.CostEstimate(
            flops=RELAYOUT_COST * bands // 64 * len(wanted) // sticks,
            transcendentals=0,
            bytes_accessed=8 * bands * len(wanted) * LANES,
        ),
        name="relayout_left" if left else "relayout_right",
    )(perm, wraps, view, *own)


def products(left, right, units, offset, size, start, finish):
    sides = (left, right)
    run = STEPS[size]
    steps = size // run
    heights = [sum(r.shape[2] for r in rows) for rows, _ in sides]
    widths = [sum(c.shape[2] for c in columns) for _, columns in sides]
    shapes = [(2 * h, 2 * w) for h, w in zip(heights, widths)]

    def stack(refs):
        return jnp.concatenate(
            [jnp.concatenate([r[c, j] for j in range(run)], -1) for c in range(2) for r in refs], 0
        )

    def body(*refs):
        refs = list(refs)
        take = lambda n: [refs.pop(0) for _ in range(n)]
        operands = [(take(len(rows)), take(len(columns))) for rows, columns in sides]
        starts = take(2) if start else None
        outs = take(1) if finish else take(2)
        totals = take(2)
        step = pl.program_id(0)

        @pl.when(step == 0)
        def _():
            for side in range(2):
                totals[side][...] = starts[side][...] if start else jnp.zeros(shapes[side], jnp.float32)

        for side, (rows, columns) in enumerate(operands):
            totals[side][...] += lax.dot_general(
                stack(rows), stack(columns), (((1,), (1,)), ((), ())), preferred_element_type=jnp.float32
            )

        @pl.when(step == steps - 1)
        def _():
            for side in range(2):
                total, h, w = totals[side], heights[side], widths[side]
                if not finish:
                    outs[side][...] = total[...]
                    continue
                real = total[:h, :w] + total[h:, w:]
                imag = total[:h, w:] - total[h:, :w]
                for part, value in enumerate((real, imag)):
                    at, to = 0, 0
                    for unit in units[side]:
                        each = unit // 8
                        for q in range(8):
                            block = value[at : at + each]
                            at += each
                            for n in range(w // LANES):
                                into = n * (h // 8) + to
                                outs[0][q, side, part, into : into + each] = block[:, n * LANES : (n + 1) * LANES]
                        to += each

    def spec(array, begin):
        return pl.BlockSpec((2, run, array.shape[2], LANES), lambda s: (0, begin // run + s, 0, 0))

    in_specs, operands = [], []
    for (rows, columns), (row_begin, column_begin) in zip(sides, ((offset, 0), (0, offset))):
        in_specs += [spec(r, row_begin) for r in rows] + [spec(c, column_begin) for c in columns]
        operands += [*rows, *columns]
    whole = [pl.BlockSpec(shape, lambda s: (0, 0)) for shape in shapes]
    if start:
        in_specs += whole
        operands += start
    if finish:
        out_shape = [(8, 2, 2, 48, LANES)]
        out_specs = [pl.BlockSpec(out_shape[0], lambda s: (0, 0, 0, 0, 0))]
    else:
        out_shape, out_specs = shapes, whole
    return pl.pallas_call(
        body,
        grid=(steps,),
        in_specs=in_specs,
        out_specs=out_specs,
        out_shape=[jax.ShapeDtypeStruct(shape, jnp.float32) for shape in out_shape],
        scratch_shapes=[pltpu.VMEM(shape, jnp.float32) for shape in shapes],
        compiler_params=PARAMS,
        cost_estimate=pl.CostEstimate(
            flops=PRODUCT_COST * 2 * size * LANES * sum(h * w for h, w in shapes),
            transcendentals=0,
            bytes_accessed=4 * size * LANES * sum(h + w for h, w in shapes),
        ),
        name="products",
    )(*operands)


def after(value, *others):
    return lax.optimization_barrier((value, others))[0]


def summed(total):
    return lax.all_to_all(total, "pw", 0, 0, tiled=True).sum(0)


def summed_apart(total):
    count = lax.axis_size("pw")
    groups = [list(range(p, count, 2)) for p in range(2)]
    pairs = total.reshape(count // 2, 2, *total.shape[1:])
    return lax.all_to_all(pairs, "pw", 0, 0, axis_index_groups=groups, tiled=True).sum(0)


def summed_near(pairs):
    side = lax.axis_index("pw") % 2
    kept = lax.dynamic_index_in_dim(pairs, side, 1, keepdims=False)
    sent = lax.dynamic_index_in_dim(pairs, 1 - side, 1, keepdims=False)
    return kept + lax.ppermute(sent, "pw", [(p, p ^ 1) for p in range(lax.axis_size("pw"))])


def shards(states, stick_perm):
    states = states[0]
    sticks = states.shape[2]
    perm = stick_perm - lax.axis_index("pw") * sticks
    token = (lax.axis_index("kz") == 0).astype(jnp.int32).reshape(1)
    own = {True: (), False: ()}
    arrivals = {True: [], False: []}
    for index, chunk in enumerate(CHUNKS):
        for left in SIDES:
            if index > 1:
                token = after(token, arrivals[left][index - 2][0])
            outs = relayout(states, perm, token, chunk, left, own[left] if index else None)
            token, outs = lax.optimization_barrier((token, outs))
            if index:
                *outs, kept = outs
                own[left] = (kept,)
            for piece in range(1, len(outs)):
                if left != SIDES[0]:
                    outs[piece] = after(outs[piece], arrivals[True][index - 1][0])
            arrivals[left].append([shifted(p, "kz", -1 if left else 1) for p in outs])
        if index == 1:
            for left in SIDES:
                own[left] = relayout(states, perm, token, CHUNKS[0], left, own[left], sends=False)
                token, own[left] = lax.optimization_barrier((token, own[left]))
    columns, rows = list(own[True]), list(own[False])
    from_right, from_left = arrivals[True], arrivals[False]

    runs = [[chunk[1]] * chunk[2] for chunk in CHUNKS]
    early = []
    for group in GROUPS:
        totals = None
        pieces = CHUNKS[group[0]][3]
        units = (sum(runs, []), sum((runs[c] for c in group), []))
        for index, size in enumerate(pieces):
            last = index == len(pieces) - 1
            arrived = [[side[c][index] for c in group] for side in (from_right, from_left)]
            if index:
                arrived, totals, early = lax.optimization_barrier((arrived, totals, early))
                near = summed_near(jnp.stack(early))
            totals = products(
                (rows, arrived[0]), (arrived[1], columns), units, sum(pieces[:index]), size, totals, last
            )
        rows, columns, totals, early = lax.optimization_barrier((rows, columns, totals, early))
        if group != GROUPS[-1]:
            early.append(summed_apart(totals[0]))
    near, totals = lax.optimization_barrier((near, totals))
    parts = jnp.concatenate([near, summed(totals[0])[None]])
    groups, _, _, height, _ = parts.shape
    from_left_part = shifted(parts[:, 1], "kz", -1).reshape(groups, 2, groups, height // groups, LANES)
    left = jnp.transpose(parts[:, 0], (2, 1, 0, 3)).reshape(height, 2, groups * LANES)
    right = jnp.transpose(from_left_part, (0, 3, 1, 2, 4)).reshape(height, 2, groups * LANES)
    return (left + right)[:, None]


def solution(mesh):
    in_specs = (P("kz", None, None, "pw", None), P("pw"))
    out_specs = P("pw", "kz", None, None)
    return jax.shard_map(shards, mesh=mesh, in_specs=in_specs, out_specs=out_specs, check_vma=False)
```

```python
import jax
import jax.numpy as jnp
from jax import lax
from jax.experimental import pallas as pl
from jax.experimental.pallas import tpu as pltpu
from jax.sharding import PartitionSpec as P

LANES = 128
CHUNKS = ((0, 64, 1, (64,)), (64, 64, 1, (64,)), (128, 64, 2, (64,)), (256, 64, 2, (48, 16)))
SIDES = (True, False)
GROUPS = ((0, 1), (2,), (3,))
STEPS = {64: 16, 48: 16, 16: 8}
RELAYOUT_COST = 5_000_000_000
PRODUCT_COST = 2
PARAMS = pltpu.CompilerParams(vmem_limit_bytes=56 << 20)


def shifted(value, axis, steps):
    count = lax.axis_size(axis)
    return lax.ppermute(value, axis, [(s, (s + steps) % count) for s in range(count)])


def relayout(states, perm, base_stick, wraps, chunk, left, own, sends=True):
    first, sub, units, pieces = chunk
    keeps = own is not None
    own = own or ()
    pitch = sub + 1
    each = sub // 8
    sticks = states.shape[2]
    half = sticks // 2
    bands = units * sub
    sent_half, kept_half = (range(half), range(half, sticks)) if left else (range(half, sticks), range(half))
    wanted = [*(sent_half if sends else ()), *(kept_half if keeps else ())]
    low = min(wanted)
    base = 0 if left else low
    pieces = pieces if sends else ()
    halves = (half,) if keeps else ()
    all_bands = states.shape[1]

    def body(perm_ref, base_ref, wraps_ref, x_ref, *refs):
        outs, scratch = refs[len(own) : -1], refs[-1]

        def spread(start, count):
            for m in range(sub):
                row = x_ref.at[0, m] if left else x_ref.at[0, m // each, m % each]
                row = row[start - base : start - base + count].astype(jnp.float32)
                scratch[pl.ds(start * pitch + m, count, stride=pitch), :] = row

        def put(s, value):
            value = value.astype(jnp.bfloat16)
            at = s % half
            if s in kept_half:
                outs[-1][0, at] = value
                return
            for piece, size in enumerate(pieces):
                if at < size:
                    outs[piece][0, at] = value
                    return
                at -= size

        def plain():
            spread(low, len(wanted))
            for s in wanted:
                put(s, scratch[pl.ds(s * pitch, sub), :])

        def wrapped():
            spread(0, sticks)
            keep = lax.broadcasted_iota(jnp.int32, (sub, LANES), 1) < LANES - 1
            for s in wanted:
                value = scratch[pl.ds((perm_ref[s] - base_ref[0]) * pitch, sub), :]
                put(s, jnp.where(keep, pltpu.roll(value, LANES - 1, 1), 0.0))

        if left:
            pl.when(wraps_ref[0] == 0)(plain)
            pl.when(wraps_ref[0] != 0)(wrapped)
        else:
            plain()

    if left:
        view = states
        in_spec = pl.BlockSpec((1, sub, sticks, LANES), lambda c, g, *_: (c, first // sub + g, 0, 0))
    else:
        view = states.reshape(2, 8, states.shape[1] // 8, sticks, LANES)
        block = (1, 8, each, len(wanted), LANES)
        in_spec = pl.BlockSpec(block, lambda c, g, *_: (c, 0, first // sub + g, low // len(wanted), 0))
    return pl.pallas_call(
        body,
        grid_spec=pltpu.PrefetchScalarGridSpec(
            num_scalar_prefetch=3,
            grid=(2, units),
            in_specs=[in_spec] + [pl.BlockSpec(memory_space=pl.ANY)] * len(own),
            out_specs=[pl.BlockSpec((1, n, sub, LANES), lambda c, g, *_: (c, 0, g, 0)) for n in pieces]
            + [pl.BlockSpec((1, n, sub, LANES), lambda c, g, *_: (c, 0, first // sub + g, 0)) for n in halves],
            scratch_shapes=[pltpu.VMEM((sticks * pitch, LANES), jnp.float32)],
        ),
        out_shape=[jax.ShapeDtypeStruct((2, n, bands, LANES), jnp.bfloat16) for n in pieces]
        + [jax.ShapeDtypeStruct((2, n, all_bands, LANES), jnp.bfloat16) for n in halves],
        input_output_aliases={4 + at: len(pieces) + at for at in range(len(own))},
        compiler_params=PARAMS,
        cost_estimate=pl.CostEstimate(
            flops=RELAYOUT_COST * bands // 64 * len(wanted) // sticks,
            transcendentals=0,
            bytes_accessed=8 * bands * len(wanted) * LANES,
        ),
        name="relayout_left" if left else "relayout_right",
    )(perm, base_stick, wraps, view, *own)


def products(left, right, units, offset, size, start, finish):
    sides = (left, right)
    run = STEPS[size]
    steps = size // run
    heights = [sum(r.shape[2] for r in rows) for rows, _ in sides]
    widths = [sum(c.shape[2] for c in columns) for _, columns in sides]
    shapes = [(2 * h, 2 * w) for h, w in zip(heights, widths)]

    def stack(refs):
        return jnp.concatenate(
            [jnp.concatenate([r[c, j] for j in range(run)], -1) for c in range(2) for r in refs], 0
        )

    def body(*refs):
        refs = list(refs)
        take = lambda n: [refs.pop(0) for _ in range(n)]
        operands = [(take(len(rows)), take(len(columns))) for rows, columns in sides]
        starts = take(2) if start else None
        outs = take(1) if finish else take(2)
        totals = take(2)
        step = pl.program_id(0)

        @pl.when(step == 0)
        def _():
            for side in range(2):
                totals[side][...] = starts[side][...] if start else jnp.zeros(shapes[side], jnp.float32)

        for side, (rows, columns) in enumerate(operands):
            totals[side][...] += lax.dot_general(
                stack(rows), stack(columns), (((1,), (1,)), ((), ())), preferred_element_type=jnp.float32
            )

        @pl.when(step == steps - 1)
        def _():
            for side in range(2):
                total, h, w = totals[side], heights[side], widths[side]
                if not finish:
                    outs[side][...] = total[...]
                    continue
                real = total[:h, :w] + total[h:, w:]
                imag = total[:h, w:] - total[h:, :w]
                for part, value in enumerate((real, imag)):
                    at, to = 0, 0
                    for unit in units[side]:
                        each = unit // 8
                        for q in range(8):
                            block = value[at : at + each]
                            at += each
                            for n in range(w // LANES):
                                into = n * (h // 8) + to
                                outs[0][q, side, part, into : into + each] = block[:, n * LANES : (n + 1) * LANES]
                        to += each

    def spec(array, begin):
        return pl.BlockSpec((2, run, array.shape[2], LANES), lambda s: (0, begin // run + s, 0, 0))

    in_specs, operands = [], []
    for (rows, columns), (row_begin, column_begin) in zip(sides, ((offset, 0), (0, offset))):
        in_specs += [spec(r, row_begin) for r in rows] + [spec(c, column_begin) for c in columns]
        operands += [*rows, *columns]
    whole = [pl.BlockSpec(shape, lambda s: (0, 0)) for shape in shapes]
    if start:
        in_specs += whole
        operands += start
    if finish:
        out_shape = [(8, 2, 2, 48, LANES)]
        out_specs = [pl.BlockSpec(out_shape[0], lambda s: (0, 0, 0, 0, 0))]
    else:
        out_shape, out_specs = shapes, whole
    return pl.pallas_call(
        body,
        grid=(steps,),
        in_specs=in_specs,
        out_specs=out_specs,
        out_shape=[jax.ShapeDtypeStruct(shape, jnp.float32) for shape in out_shape],
        scratch_shapes=[pltpu.VMEM(shape, jnp.float32) for shape in shapes],
        compiler_params=PARAMS,
        cost_estimate=pl.CostEstimate(
            flops=PRODUCT_COST * 2 * size * LANES * sum(h * w for h, w in shapes),
            transcendentals=0,
            bytes_accessed=4 * size * LANES * sum(h + w for h, w in shapes),
        ),
        name="products",
    )(*operands)


def after(value, *others):
    return lax.optimization_barrier((value, others))[0]


def summed(total):
    return lax.all_to_all(total, "pw", 0, 0, tiled=True).sum(0)


def summed_apart(total):
    count = lax.axis_size("pw")
    groups = [list(range(p, count, 2)) for p in range(2)]
    pairs = total.reshape(count // 2, 2, *total.shape[1:])
    return lax.all_to_all(pairs, "pw", 0, 0, axis_index_groups=groups, tiled=True).sum(0)


def summed_near(pairs):
    side = lax.axis_index("pw") % 2
    kept = lax.dynamic_index_in_dim(pairs, side, 1, keepdims=False)
    sent = lax.dynamic_index_in_dim(pairs, 1 - side, 1, keepdims=False)
    return kept + lax.ppermute(sent, "pw", [(p, p ^ 1) for p in range(lax.axis_size("pw"))])


def shards(states, stick_perm):
    states = states[0]
    sticks = states.shape[2]
    base_stick = (lax.axis_index("pw") * sticks).astype(jnp.int32).reshape(1)
    token = (lax.axis_index("kz") == 0).astype(jnp.int32).reshape(1)
    own = {True: (), False: ()}
    arrivals = {True: [], False: []}
    for index, chunk in enumerate(CHUNKS):
        for left in SIDES:
            if index > 1:
                token = after(token, arrivals[left][index - 2][0])
            outs = relayout(states, stick_perm, base_stick, token, chunk, left, own[left] if index else None)
            token, outs = lax.optimization_barrier((token, outs))
            if index:
                *outs, kept = outs
                own[left] = (kept,)
            for piece in range(1, len(outs)):
                if left != SIDES[0]:
                    outs[piece] = after(outs[piece], arrivals[True][index - 1][0])
            arrivals[left].append([shifted(p, "kz", -1 if left else 1) for p in outs])
        if index == 1:
            for left in SIDES:
                own[left] = relayout(states, stick_perm, base_stick, token, CHUNKS[0], left, own[left], sends=False)
                token, own[left] = lax.optimization_barrier((token, own[left]))
    columns, rows = list(own[True]), list(own[False])
    from_right, from_left = arrivals[True], arrivals[False]

    runs = [[chunk[1]] * chunk[2] for chunk in CHUNKS]
    early = []
    for group in GROUPS:
        totals = None
        pieces = CHUNKS[group[0]][3]
        units = (sum(runs, []), sum((runs[c] for c in group), []))
        for index, size in enumerate(pieces):
            last = index == len(pieces) - 1
            arrived = [[side[c][index] for c in group] for side in (from_right, from_left)]
            if index:
                arrived, totals, early = lax.optimization_barrier((arrived, totals, early))
                near = summed_near(jnp.stack(early))
            totals = products(
                (rows, arrived[0]), (arrived[1], columns), units, sum(pieces[:index]), size, totals, last
            )
        rows, columns, totals, early = lax.optimization_barrier((rows, columns, totals, early))
        if group != GROUPS[-1]:
            early.append(summed_apart(totals[0]))
    near, totals = lax.optimization_barrier((near, totals))
    parts = jnp.concatenate([near, summed(totals[0])[None]])
    groups, _, _, height, _ = parts.shape
    from_left_part = shifted(parts[:, 1], "kz", -1).reshape(groups, 2, groups, height // groups, LANES)
    left = jnp.transpose(parts[:, 0], (2, 1, 0, 3)).reshape(height, 2, groups * LANES)
    right = jnp.transpose(from_left_part, (0, 3, 1, 2, 4)).reshape(height, 2, groups * LANES)
    return (left + right)[:, None]


def solution(mesh):
    in_specs = (P("kz", None, None, "pw", None), P("pw"))
    out_specs = P("pw", "kz", None, None)
    return jax.shard_map(shards, mesh=mesh, in_specs=in_specs, out_specs=out_specs, check_vma=False)
```
